512 devices in a mesh: aux: 8 (over z), ao: 16 (over y, core), orb: 4 (over x).
Axes of the slice: x: 4, y: 8, z: 8, core: 2. Of those that a mesh axis runs over, the one named last changes fastest.
Arguments:
- integrals: bfloat16 [128, 16, 4, 128, 128], P('aux', 'ao', None, 'orb'), may hold values from -6 to 6
- partner: int32 [16, 4], P('ao'), may hold values from 0 to 15
- pair_count: int32 [16], P('ao'), may hold values from 1 to 4
- occupied_coeff: bfloat16 [2048, 512], P('ao', 'orb'), may hold values from -0.25 to 0.25
- occupied_domain: int32 [16, 4], P('ao', 'orb'), may hold values 0 or 1
- virtual_coeff: bfloat16 [2048, 8192], P('aux', 'ao'), may hold values from -0.125 to 0.125
- virtual_domain: int32 [16, 64], P(None, 'ao'), may hold values 0 or 1
Outputs:
- transformed: bfloat16 [128, 512, 8192], P('aux', 'orb', 'ao')
The draws below stay inside these ranges and needn't reach their ends.
All inputs are finite; a program needn't handle non-finite values. No bound on the sum of `occupied_domain` or of `virtual_domain` on one device may be relied on, other than what follows from the above.
Results may differ from the reference program's by a relative error of at most 0.0049.
Values may be sent and summed in bfloat16 or wider, within the bound.
A program may use at most 64 MiB of HBM per device.

```python
import jax
import jax.numpy as jnp
from jax import lax

BLK = 128
K = 4
AUX = 128
NBLK = 16
NAO = 2048
NOCC = 512
NVIR = 8192
NOCB = 4
NVB = 64


def place_ends(drawn, stream_key, low, high):
    index_at = [jax.random.randint(jax.random.fold_in(stream_key, axis), (), 0, length) for axis, length in enumerate(drawn.shape)]
    main_axis = drawn.shape.index(max(drawn.shape))
    neighbour = index_at[:main_axis] + [(index_at[main_axis] + 1) % drawn.shape[main_axis]] + index_at[main_axis + 1:]
    return drawn.at[tuple(index_at)].set(low).at[tuple(neighbour)].set(high)


def shard_levels(own_key, shape, shards, least, high):
    def one(position, blocks):
        draws = jax.random.uniform(jax.random.fold_in(jax.random.fold_in(own_key, 6), position), (blocks,), jnp.float32, least / len(shards), high / len(shards))
        return jnp.repeat(jnp.exp(draws), shape[position] // blocks).reshape((-1,) + (1,) * (len(shape) - position - 1))

    factor_of = one(*shards[0])
    for cut in shards[1:]:
        factor_of = factor_of * one(*cut)
    return factor_of


def noise(stream_key, extent, spread, limit, split=(), kind=jnp.bfloat16):
    entries = spread * jax.random.normal(stream_key, extent, jnp.float32)
    if split:
        entries = entries * shard_levels(stream_key, extent, split, -0.22, 0.18)
    return jnp.clip(entries, -limit, limit).astype(kind)


def setup_inputs(seed: int = 0) -> dict:
    seeds = jax.random.split(jax.random.key(seed), 8)
    integrals = noise(seeds[0], (AUX, NBLK, K, BLK, BLK), 1.0, 6.0, ((0, 8), (1, 16), (3, 4)))
    partner = place_ends(jax.random.randint(seeds[1], (NBLK, K), 0, NBLK), jax.random.fold_in(seeds[1], 1), 0, NBLK - 1).astype(jnp.int32)
    pair_count = place_ends(jax.random.randint(seeds[2], (NBLK,), 1, K + 1), jax.random.fold_in(seeds[2], 1), 1, K).astype(jnp.int32)
    occupied_coeff = noise(seeds[3], (NAO, NOCC), (K * BLK) ** -0.5, 0.25, ((0, 16), (1, 4)))
    occupied_domain = place_ends((jax.random.randint(seeds[4], (NBLK, NOCB), 0, 4) < 3).astype(jnp.int32), jax.random.fold_in(seeds[4], 1), 0, 1)
    virtual_coeff = noise(seeds[5], (NAO, NVIR), NAO ** -0.5, 0.125, ((0, 8), (1, 16)))
    virtual_domain = place_ends((jax.random.randint(seeds[6], (NBLK, NVB), 0, 4) < 3).astype(jnp.int32), jax.random.fold_in(seeds[6], 1), 0, 1)
    return dict(integrals=integrals, partner=partner, pair_count=pair_count, occupied_coeff=occupied_coeff, occupied_domain=occupied_domain, virtual_coeff=virtual_coeff, virtual_domain=virtual_domain)


def reference(integrals, partner, pair_count, occupied_coeff, occupied_domain, virtual_coeff, virtual_domain):
    occ_mask = jnp.repeat(jnp.repeat(occupied_domain, BLK, axis=0), BLK, axis=1).astype(jnp.bfloat16)
    occupied_masked = occupied_coeff * occ_mask
    vir_mask = jnp.repeat(jnp.repeat(virtual_domain, BLK, axis=0), BLK, axis=1).astype(jnp.bfloat16)
    virtual_masked = virtual_coeff * vir_mask
    blocks = occupied_masked.reshape(NBLK, BLK, NOCC)[partner]
    slots = jnp.arange(K, dtype=jnp.int32)
    live = (slots[None, :] < pair_count[:, None]).astype(jnp.float32)
    blocks_wide = blocks.astype(jnp.float32) * live[:, :, None, None]

    def one_row(slab):
        half = jnp.einsum('nkri,nkrv->inv', blocks_wide, slab.astype(jnp.float32))
        half = half.reshape(NOCC, NAO).astype(jnp.bfloat16)
        return jnp.dot(half, virtual_masked, preferred_element_type=jnp.float32).astype(jnp.bfloat16)

    return lax.map(one_row, integrals)
```

```python
import jax
import jax.numpy as jnp
from jax import lax
from jax.sharding import PartitionSpec as P


def local(
    integrals, partner, pair_count, occupied_coeff, occupied_domain, virtual_coeff, virtual_domain
):
    block_size = integrals.shape[4]
    slab_rows = integrals.shape[0]
    slot_count = integrals.shape[2]
    occ_width = occupied_coeff.shape[1]
    occ_local = occupied_coeff * occupied_domain.astype(jnp.bfloat16)
    all_occ = lax.all_gather(occ_local, "ao", axis=0, tiled=True)
    all_ints = lax.all_gather(integrals, "orb", axis=3, tiled=True)

    vir_blocks = virtual_coeff.shape[0] // block_size
    first = lax.axis_index("aux") * vir_blocks
    dom = lax.dynamic_slice_in_dim(virtual_domain, first, vir_blocks, axis=0).astype(jnp.bfloat16)
    dom = jnp.repeat(jnp.repeat(dom, block_size, axis=0), block_size, axis=1)
    vir_masked = lax.all_gather(virtual_coeff * dom, "aux", axis=0, tiled=True)

    picked = all_occ.reshape(-1, block_size, occ_width)[partner[0]]
    slots = jnp.arange(slot_count, dtype=jnp.int32)
    live = (slots < pair_count[0]).astype(jnp.bfloat16)
    picked = picked * live[:, None, None]
    half = jnp.einsum(
        "kri,pkrv->piv", picked, all_ints[:, 0], preferred_element_type=jnp.float32
    ).astype(jnp.bfloat16)
    piece = lax.all_gather(half, "ao", axis=2, tiled=True)
    flat = piece.reshape(slab_rows * occ_width, piece.shape[2])
    product = jnp.dot(flat, vir_masked, preferred_element_type=jnp.float32)
    return product.reshape(slab_rows, occ_width, -1).astype(jnp.bfloat16)


def solution(mesh):
    placed = (
        P("aux", "ao", None, "orb", None),
        P("ao", None),
        P("ao"),
        P("ao", "orb"),
        P("ao", "orb"),
        P("aux", "ao"),
        P(None, "ao"),
    )
    return jax.shard_map(
        local, mesh=mesh, in_specs=placed, out_specs=P("aux", "orb", "ao"), check_vma=False
    )
```

```python
import functools

import jax
import jax.numpy as jnp
from jax import lax
from jax.experimental import pallas as pl
from jax.experimental.pallas import tpu as pltpu
from jax.sharding import PartitionSpec as P

MESH = pl.DeviceIdType.MESH
CHUNKS = 4


class Keys:
    def __init__(self):
        self.index = {}

    def __getitem__(self, key):
        return self.index.setdefault(key, len(self.index))


def kernel(
    size, chunks, occ, ints, vir, partner, count, vdom, out,
    occ_all, from_left, from_right, from_far, spread, half, vir_all, vir_masked, staged,
    send_sem, recv_sem, out_sem,
):
    nz, ny, nx = size
    slab, slots, rows, width = ints.shape
    per = slab // chunks
    keys = Keys()
    pending = []

    z, me, x = lax.axis_index("aux"), lax.axis_index("ao"), lax.axis_index("orb")
    y, core = me // 2, me % 2
    sibling = {"ao": y * 2 + 1 - core}

    def around(axis, delta):
        if axis == "aux":
            return {"aux": (z + delta + nz) % nz}
        if axis == "orb":
            return {"orb": (x + delta + nx) % nx}
        return {"ao": ((y + delta + ny) % ny) * 2 + core}

    def block(delta, same=True):
        return ((y + delta + ny) % ny) * 2 + (core if same else 1 - core)

    def copy(key, src, dst, device):
        i = keys[key]
        return pltpu.make_async_remote_copy(
            src_ref=src, dst_ref=dst, send_sem=send_sem.at[i], recv_sem=recv_sem.at[i],
            device_id=device, device_id_type=MESH,
        )

    def post(key, src, dst, device):
        c = copy(key, src, dst, device)
        c.start()
        pending.append(c)

    def arrive(key, dst, device=sibling):
        copy(key, dst, dst, device).wait_recv()

    barrier = pltpu.get_barrier_semaphore()
    peers = [around("orb", 1), around("orb", -1), around("aux", 1), around("aux", -1), sibling]
    peers += [around("ao", d) for d in range(1, ny)]
    for peer in peers:
        pl.semaphore_signal(barrier, inc=1, device_id=peer, device_id_type=MESH)
    pl.semaphore_wait(barrier, len(peers))

    def part(c):
        return pl.ds(c * per, per)

    def ints_own(c):
        post(("x", "R", c), ints.at[part(c)], from_left.at[part(c)], around("orb", 1))
        post(("x", "L", c), ints.at[part(c)], from_right.at[part(c)], around("orb", -1))

    def ints_step(c):
        arrive(("x", "R", c), from_left.at[part(c)])
        arrive(("x", "L", c), from_right.at[part(c)])
        if c % 2 == 0:
            post(("x", "D", c), from_left.at[part(c)], from_far.at[part(c)], around("orb", 1))
        else:
            post(("x", "D", c), from_right.at[part(c)], from_far.at[part(c)], around("orb", -1))
        if c + 2 < chunks:
            ints_own(c + 2)

    ints_own(0)
    for d in (1, 7, 2, 6, 3, 5, 4):
        post(("o", d), occ, occ_all.at[me], around("ao", d))
    post(("os", 0), occ, occ_all.at[me], sibling)
    ints_own(1)
    for h in range(2):
        post(("v", "R", 1, h), vir.at[h], vir_all.at[z * 2 + h], around("aux", 1))
        post(("v", "L", 1, h), vir.at[h], vir_all.at[z * 2 + h], around("aux", -1))
    occ_all[me] = occ[...]
    for h in range(2):
        vir_all[z * 2 + h] = vir[h]

    ints_step(0)
    for d in (1, 7, 2, 6, 3, 5, 4):
        slot = occ_all.at[block(-d)]
        arrive(("o", d), slot)
        post(("os", d), slot, slot, sibling)
    for d in (0, 1, 7, 2, 6, 3, 5, 4):
        arrive(("os", d), occ_all.at[block(-d, False)])

    pieces = []
    for rel in (0, -1, 1, 2):
        first = pl.multiple_of(((x + rel + nx) % nx) * rows, rows)
        for k in range(slots):
            live = jnp.where(k < count[0], 1.0, 0.0).astype(jnp.float32)
            picked = occ_all[partner[0, k], pl.ds(first, rows), :].astype(jnp.float32)
            pieces.append(picked * live)
    spread[...] = jnp.concatenate(pieces, axis=0).T.astype(jnp.bfloat16)

    def half_step(c):
        arrive(("x", "D", c), from_far.at[part(c)])
        columns = []
        for p in range(c * per, (c + 1) * per):
            columns.append(
                jnp.concatenate(
                    [
                        ref[p].reshape(slots * rows, width)
                        for ref in (ints, from_left, from_right, from_far)
                    ],
                    axis=0,
                )
            )
        res = jnp.dot(
            spread[...], jnp.concatenate(columns, axis=1), preferred_element_type=jnp.float32
        ).astype(jnp.bfloat16)
        for j in range(per):
            half[me, c * per + j] = res[:, j * width : (j + 1) * width]
        own = half.at[me, part(c)]
        post(("y", "R", 1, c), own, own, around("ao", 1))
        post(("y", "L", 1, c), own, own, around("ao", -1))
        post(("s", "O", 0, c), own, own, sibling)

    def routes(d, c):
        far = ny // 2
        if d < far:
            return ("R", "L")
        if d > far:
            return ()
        return ("R",) if c % 2 == 0 else ("L",)

    def half_pass(d, c):
        for way in routes(d, c):
            sign = 1 if way == "R" else -1
            slot = half.at[block(-sign * d), part(c)]
            arrive(("y", way, d, c), slot)
            if way in routes(d + 1, c):
                post(("y", way, d + 1, c), slot, slot, around("ao", sign))
            post(("s", way, d, c), slot, slot, sibling)

    def vir_pass(d):
        for h in range(2):
            for way in routes(d, h):
                sign = 1 if way == "R" else -1
                slot = vir_all.at[((z - sign * d + nz) % nz) * 2 + h]
                arrive(("v", way, d, h), slot)
                if way in routes(d + 1, h):
                    post(("v", way, d + 1, h), slot, slot, around("aux", sign))

    def mask():
        def body(m, carry):
            for b in range(vdom.shape[1]):
                on = jnp.full((width, width), vdom[m, b].astype(jnp.float32)).astype(jnp.bfloat16)
                at = slice(b * width, (b + 1) * width)
                first = pl.multiple_of(m * width, width)
                vir_masked[pl.ds(first, width), at] = vir_all[m, :, at] * on
            return carry

        lax.fori_loop(0, vir_all.shape[0], body, 0)

    def drain(c):
        arrive(("s", "O", 0, c), half.at[block(0, False), part(c)])
        for d in range(1, ny // 2 + 1):
            for way in routes(d, c):
                sign = 1 if way == "R" else -1
                arrive(("s", way, d, c), half.at[block(-sign * d, False), part(c)])

    def multiply(c):
        blocks = half.shape[0]

        def body(t, carry):
            p = c * per + t * 2
            lhs = jnp.concatenate(
                [half[n, pl.ds(p, 2)].reshape(2 * width, width) for n in range(blocks)], axis=1
            )
            res = jnp.dot(lhs, vir_masked[...], preferred_element_type=jnp.float32)
            staged[pl.ds(p, 2)] = res.astype(jnp.bfloat16).reshape(2, width, -1)
            return carry

        lax.fori_loop(0, per // 2, body, 0)
        done = pltpu.make_async_copy(staged.at[part(c)], out.at[part(c)], out_sem.at[c])
        done.start()
        return done

    outs = []
    far = ny // 2
    for s in range(chunks + far):
        if s + 1 < chunks:
            ints_step(s + 1)
        if s < chunks:
            half_step(s)
        if s < far:
            vir_pass(s + 1)
        for d in range(1, far + 1):
            if 0 <= s - d < chunks:
                half_pass(d, s - d)
        if s == far:
            mask()
        if s >= far:
            drain(s - far)
            outs.append(multiply(s - far))
    for c in pending:
        c.wait_send()
    for c in outs:
        c.wait()


def copies(chunks):
    return 18 * chunks + 29


def local(size, integrals, partner, pair_count, occ_coeff, occ_domain, vir_coeff, vir_domain):
    slab, _, slots, rows, width = integrals.shape
    nz, ny, nx = size
    blocks = 2 * ny
    occ_width = occ_coeff.shape[1]
    vir_width = vir_coeff.shape[1]
    occ = occ_coeff * occ_domain.astype(jnp.bfloat16)
    ints = integrals.reshape(slab, slots, rows, width)
    vir = vir_coeff.reshape(-1, width, vir_width)
    n = copies(CHUNKS)
    vmem = pl.BlockSpec(memory_space=pltpu.VMEM)
    smem = pl.BlockSpec(memory_space=pltpu.SMEM)
    return pl.pallas_call(
        functools.partial(kernel, size, CHUNKS),
        out_shape=jax.ShapeDtypeStruct((slab, occ_width, vir_width), jnp.bfloat16),
        in_specs=[vmem] * 3 + [smem] * 3,
        out_specs=pl.BlockSpec(memory_space=pl.ANY),
        scratch_shapes=[
            pltpu.VMEM((blocks, width, occ_width), jnp.bfloat16),
            pltpu.VMEM(ints.shape, jnp.bfloat16),
            pltpu.VMEM(ints.shape, jnp.bfloat16),
            pltpu.VMEM(ints.shape, jnp.bfloat16),
            pltpu.VMEM((occ_width, nx * slots * rows), jnp.bfloat16),
            pltpu.VMEM((blocks, slab, occ_width, width), jnp.bfloat16),
            pltpu.VMEM((blocks, width, vir_width), jnp.bfloat16),
            pltpu.VMEM((blocks * width, vir_width), jnp.bfloat16),
            pltpu.VMEM((slab, occ_width, vir_width), jnp.bfloat16),
            pltpu.SemaphoreType.DMA((n,)),
            pltpu.SemaphoreType.DMA((n,)),
            pltpu.SemaphoreType.DMA((CHUNKS,)),
        ],
        compiler_params=pltpu.CompilerParams(
            collective_id=0, has_side_effects=True, vmem_limit_bytes=60 * 1024 * 1024
        ),
    )(occ, ints, vir, partner, pair_count, vir_domain)


def solution(mesh):
    size = (mesh.shape["aux"], mesh.shape["ao"] // 2, mesh.shape["orb"])
    placed = (
        P("aux", "ao", None, "orb", None),
        P("ao", None),
        P("ao"),
        P("ao", "orb"),
        P("ao", "orb"),
        P("aux", "ao"),
        P(None, "ao"),
    )
    return jax.shard_map(
        functools.partial(local, size), mesh=mesh, in_specs=placed,
        out_specs=P("aux", "orb", "ao"), check_vma=False,
    )
```

```python
import functools

import jax
import jax.numpy as jnp
from jax import lax
from jax.experimental import pallas as pl
from jax.experimental.pallas import tpu as pltpu
from jax.sharding import PartitionSpec as P

MESH = pl.DeviceIdType.MESH
CHUNKS = (4, 4, 4, 4)
VIR_STEPS = (1, 2, 3, 4)


class Keys:
    def __init__(self):
        self.index = {}

    def __getitem__(self, key):
        return self.index.setdefault(key, len(self.index))


def kernel(
    size, sizes, vir_steps, occ, ints, vir, partner, count, odom, vdom, out,
    occ_all, from_left, from_right, from_far, spread, half, vir_all, vir_masked, staged,
    send_sem, recv_sem, out_sem,
):
    nz, ny, nx = size
    slab, slots, rows, width = ints.shape
    chunks = len(sizes)
    firsts = [sum(sizes[:c]) for c in range(chunks)]
    keys = Keys()
    pending = []

    z, me, x = lax.axis_index("aux"), lax.axis_index("ao"), lax.axis_index("orb")
    y, core = me // 2, me % 2
    sibling = {"ao": y * 2 + 1 - core}

    def around(axis, delta):
        if axis == "aux":
            return {"aux": (z + delta + nz) % nz}
        if axis == "orb":
            return {"orb": (x + delta + nx) % nx}
        return {"ao": ((y + delta + ny) % ny) * 2 + core}

    def block(delta, same=True):
        return ((y + delta + ny) % ny) * 2 + (core if same else 1 - core)

    def copy(key, src, dst, device):
        i = keys[key]
        return pltpu.make_async_remote_copy(
            src_ref=src, dst_ref=dst, send_sem=send_sem.at[i], recv_sem=recv_sem.at[i],
            device_id=device, device_id_type=MESH,
        )

    def post(key, src, dst, device):
        c = copy(key, src, dst, device)
        c.start()
        pending.append(c)

    def arrive(key, dst, device=sibling):
        copy(key, dst, dst, device).wait_recv()

    keep = jnp.full(occ.shape, odom[0, 0].astype(jnp.float32)).astype(jnp.bfloat16)
    occ_all[me] = occ[...] * keep
    for h in range(2):
        vir_all[z * 2 + h] = vir[h]

    barrier = pltpu.get_barrier_semaphore()
    peers = [around("orb", 1), around("orb", -1), around("aux", 1), around("aux", -1), sibling]
    peers += [around("ao", d) for d in range(1, ny)]
    for peer in peers:
        pl.semaphore_signal(barrier, inc=1, device_id=peer, device_id_type=MESH)
    pl.semaphore_wait(barrier, len(peers))

    def part(c):
        return pl.ds(firsts[c], sizes[c])

    def ints_own(c):
        post(("x", "R", c), ints.at[part(c)], from_left.at[part(c)], around("orb", 1))
        post(("x", "L", c), ints.at[part(c)], from_right.at[part(c)], around("orb", -1))

    def ints_step(c):
        arrive(("x", "R", c), from_left.at[part(c)])
        arrive(("x", "L", c), from_right.at[part(c)])
        if c % 2 == 0:
            post(("x", "D", c), from_left.at[part(c)], from_far.at[part(c)], around("orb", 1))
        else:
            post(("x", "D", c), from_right.at[part(c)], from_far.at[part(c)], around("orb", -1))
        if c + 2 < chunks:
            ints_own(c + 2)

    ints_own(0)
    for d in (1, 7, 2, 6, 3, 5, 4):
        post(("o", d), occ_all.at[me], occ_all.at[me], around("ao", d))
    post(("os", 0), occ_all.at[me], occ_all.at[me], sibling)
    ints_own(1)
    for h in range(2):
        post(("v", "R", 1, h), vir.at[h], vir_all.at[z * 2 + h], around("aux", 1))
        post(("v", "L", 1, h), vir.at[h], vir_all.at[z * 2 + h], around("aux", -1))

    ints_step(0)
    for d in (1, 7, 2, 6, 3, 5, 4):
        slot = occ_all.at[block(-d)]
        arrive(("o", d), slot)
        post(("os", d), slot, slot, sibling)
    ints_step(1)
    for d in (0, 1, 7, 2, 6, 3, 5, 4):
        arrive(("os", d), occ_all.at[block(-d, False)])

    pieces = []
    for rel in (0, -1, 1, 2):
        first = pl.multiple_of(((x + rel + nx) % nx) * rows, rows)
        for k in range(slots):
            live = jnp.where(k < count[0], 1.0, 0.0).astype(jnp.float32)
            picked = occ_all[partner[0, k], pl.ds(first, rows), :].astype(jnp.float32)
            pieces.append(picked * live)
    spread[...] = jnp.concatenate(pieces, axis=0).T.astype(jnp.bfloat16)

    def half_step(c):
        arrive(("x", "D", c), from_far.at[part(c)])
        columns = []
        for p in range(firsts[c], firsts[c] + sizes[c]):
            columns.append(
                jnp.concatenate(
                    [
                        ref[p].reshape(slots * rows, width)
                        for ref in (ints, from_left, from_right, from_far)
                    ],
                    axis=0,
                )
            )
        res = jnp.dot(
            spread[...], jnp.concatenate(columns, axis=1), preferred_element_type=jnp.float32
        ).astype(jnp.bfloat16)
        for j in range(sizes[c]):
            half[me, firsts[c] + j] = res[:, j * width : (j + 1) * width]
        own = half.at[me, part(c)]
        post(("y", "R", 1, c), own, own, around("ao", 1))
        post(("y", "L", 1, c), own, own, around("ao", -1))
        post(("s", "O", 0, c), own, own, sibling)

    def routes(d, c):
        far = ny // 2
        if d < far:
            return ("R", "L")
        if d > far:
            return ()
        return ("R",) if c % 2 == 0 else ("L",)

    def half_pass(d, c):
        for way in routes(d, c):
            sign = 1 if way == "R" else -1
            slot = half.at[block(-sign * d), part(c)]
            arrive(("y", way, d, c), slot)
            if way in routes(d + 1, c):
                post(("y", way, d + 1, c), slot, slot, around("ao", sign))
            post(("s", way, d, c), slot, slot, sibling)

    def vir_pass(d):
        for h in range(2):
            for way in routes(d, h):
                sign = 1 if way == "R" else -1
                slot = vir_all.at[((z - sign * d + nz) % nz) * 2 + h]
                arrive(("v", way, d, h), slot)
                if way in routes(d + 1, h):
                    post(("v", way, d + 1, h), slot, slot, around("aux", sign))

    def mask():
        def body(m, carry):
            for b in range(vdom.shape[0]):
                on = jnp.full((width, width), vdom[b, m].astype(jnp.float32)).astype(jnp.bfloat16)
                at = slice(b * width, (b + 1) * width)
                first = pl.multiple_of(m * width, width)
                vir_masked[pl.ds(first, width), at] = vir_all[m, :, at] * on
            return carry

        lax.fori_loop(0, vir_all.shape[0], body, 0)

    def drain(c):
        arrive(("s", "O", 0, c), half.at[block(0, False), part(c)])
        for d in range(1, ny // 2 + 1):
            for way in routes(d, c):
                sign = 1 if way == "R" else -1
                arrive(("s", way, d, c), half.at[block(-sign * d, False), part(c)])

    def multiply(c):
        blocks = half.shape[0]

        def body(t, carry):
            p = firsts[c] + t * 2
            lhs = jnp.concatenate(
                [half[n, pl.ds(p, 2)].reshape(2 * width, width) for n in range(blocks)], axis=1
            )
            res = jnp.dot(lhs, vir_masked[...], preferred_element_type=jnp.float32)
            staged[pl.ds(p, 2)] = res.astype(jnp.bfloat16).reshape(2, width, -1)
            return carry

        lax.fori_loop(0, sizes[c] // 2, body, 0)
        done = pltpu.make_async_copy(staged.at[part(c)], out.at[part(c)], out_sem.at[c])
        done.start()
        return done

    outs = []
    far = ny // 2
    for s in range(chunks + far):
        if 1 < s + 1 < chunks:
            ints_step(s + 1)
        if s < chunks:
            half_step(s)
        for d in range(1, far + 1):
            if 0 <= s - d < chunks:
                half_pass(d, s - d)
        for d in range(1, far + 1):
            if s == vir_steps[d - 1]:
                vir_pass(d)
        if s == vir_steps[-1]:
            mask()
        if s >= max(far, vir_steps[-1]):
            while len(outs) <= s - far:
                drain(len(outs))
                outs.append(multiply(len(outs)))
    for c in pending:
        c.wait_send()
    for c in outs:
        c.wait()


def copies(chunks):
    return 18 * chunks + 29


def local(size, integrals, partner, pair_count, occ_coeff, occ_domain, vir_coeff, vir_domain):
    slab, _, slots, rows, width = integrals.shape
    nz, ny, nx = size
    blocks = 2 * ny
    occ_width = occ_coeff.shape[1]
    vir_width = vir_coeff.shape[1]
    ints = integrals.reshape(slab, slots, rows, width)
    vir = vir_coeff.reshape(-1, width, vir_width)
    n = copies(len(CHUNKS))
    vmem = pl.BlockSpec(memory_space=pltpu.VMEM)
    smem = pl.BlockSpec(memory_space=pltpu.SMEM)
    return pl.pallas_call(
        functools.partial(kernel, size, CHUNKS, VIR_STEPS),
        out_shape=jax.ShapeDtypeStruct((slab, occ_width, vir_width), jnp.bfloat16),
        in_specs=[vmem] * 3 + [smem] * 4,
        out_specs=pl.BlockSpec(memory_space=pl.ANY),
        scratch_shapes=[
            pltpu.VMEM((blocks, width, occ_width), jnp.bfloat16),
            pltpu.VMEM(ints.shape, jnp.bfloat16),
            pltpu.VMEM(ints.shape, jnp.bfloat16),
            pltpu.VMEM(ints.shape, jnp.bfloat16),
            pltpu.VMEM((occ_width, nx * slots * rows), jnp.bfloat16),
            pltpu.VMEM((blocks, slab, occ_width, width), jnp.bfloat16),
            pltpu.VMEM((blocks, width, vir_width), jnp.bfloat16),
            pltpu.VMEM((blocks * width, vir_width), jnp.bfloat16),
            pltpu.VMEM((slab, occ_width, vir_width), jnp.bfloat16),
            pltpu.SemaphoreType.DMA((n,)),
            pltpu.SemaphoreType.DMA((n,)),
            pltpu.SemaphoreType.DMA((len(CHUNKS),)),
        ],
        compiler_params=pltpu.CompilerParams(
            collective_id=0, has_side_effects=True, vmem_limit_bytes=30 * 1024 * 1024
        ),
    )(occ_coeff, ints, vir, partner, pair_count, occ_domain, vir_domain.T)


def solution(mesh):
    size = (mesh.shape["aux"], mesh.shape["ao"] // 2, mesh.shape["orb"])
    placed = (
        P("aux", "ao", None, "orb", None),
        P("ao", None),
        P("ao"),
        P("ao", "orb"),
        P("ao", "orb"),
        P("aux", "ao"),
        P(None, "ao"),
    )
    return jax.shard_map(
        functools.partial(local, size), mesh=mesh, in_specs=placed,
        out_specs=P("aux", "orb", "ao"), check_vma=False,
    )
```

```python
import functools

import jax
import jax.numpy as jnp
from jax import lax
from jax.experimental import pallas as pl
from jax.experimental.pallas import tpu as pltpu
from jax.sharding import PartitionSpec as P

MESH = pl.DeviceIdType.MESH
CHUNKS = (4, 4, 4, 4)
VIR_STEPS = (1, 2, 3, 4)


class Keys:
    def __init__(self):
        self.index = {}

    def __getitem__(self, key):
        return self.index.setdefault(key, len(self.index))


def kernel(
    size, sizes, vir_steps, occ, ints, vir, partner, count, odom, vdom, out,
    occ_all, from_left, from_right, from_far, spread, half, vir_all, vir_masked, staged, total,
    send_sem, recv_sem, out_sem,
):
    nz, ny, nx = size
    slab, slots, rows, width = ints.shape
    chunks = len(sizes)
    firsts = [sum(sizes[:c]) for c in range(chunks)]
    keys = Keys()
    pending = []

    z, me, x = lax.axis_index("aux"), lax.axis_index("ao"), lax.axis_index("orb")
    y, core = me // 2, me % 2
    sibling = {"ao": y * 2 + 1 - core}

    def around(axis, delta):
        if axis == "aux":
            return {"aux": (z + delta + nz) % nz}
        if axis == "orb":
            return {"orb": (x + delta + nx) % nx}
        return {"ao": ((y + delta + ny) % ny) * 2 + core}

    def block(delta, same=True):
        return ((y + delta + ny) % ny) * 2 + (core if same else 1 - core)

    def copy(key, src, dst, device):
        i = keys[key]
        return pltpu.make_async_remote_copy(
            src_ref=src, dst_ref=dst, send_sem=send_sem.at[i], recv_sem=recv_sem.at[i],
            device_id=device, device_id_type=MESH,
        )

    def post(key, src, dst, device):
        c = copy(key, src, dst, device)
        c.start()
        pending.append(c)

    def arrive(key, dst, device=sibling):
        copy(key, dst, dst, device).wait_recv()

    keep = jnp.full(occ.shape, odom[0, 0].astype(jnp.float32)).astype(jnp.bfloat16)
    occ_all[me] = occ[...] * keep
    for h in range(2):
        vir_all[z * 2 + h] = vir[h]

    barrier = pltpu.get_barrier_semaphore()
    peers = [around("orb", 1), around("orb", -1), around("aux", 1), around("aux", -1), sibling]
    peers += [around("ao", d) for d in range(1, ny)]
    for peer in peers:
        pl.semaphore_signal(barrier, inc=1, device_id=peer, device_id_type=MESH)
    pl.semaphore_wait(barrier, len(peers))

    def part(c):
        return pl.ds(firsts[c], sizes[c])

    def ints_own(c):
        post(("x", "R", c), ints.at[part(c)], from_left.at[part(c)], around("orb", 1))
        post(("x", "L", c), ints.at[part(c)], from_right.at[part(c)], around("orb", -1))

    def ints_step(c):
        arrive(("x", "R", c), from_left.at[part(c)])
        arrive(("x", "L", c), from_right.at[part(c)])
        if c % 2 == 0:
            post(("x", "D", c), from_left.at[part(c)], from_far.at[part(c)], around("orb", 1))
        else:
            post(("x", "D", c), from_right.at[part(c)], from_far.at[part(c)], around("orb", -1))
        if c + 2 < chunks:
            ints_own(c + 2)

    ints_own(0)
    for d in (1, 7, 2, 6, 3, 5, 4):
        post(("o", d), occ_all.at[me], occ_all.at[me], around("ao", d))
    post(("os", 0), occ_all.at[me], occ_all.at[me], sibling)
    ints_own(1)
    for h in range(2):
        post(("v", "R", 1, h), vir.at[h], vir_all.at[z * 2 + h], around("aux", 1))
        post(("v", "L", 1, h), vir.at[h], vir_all.at[z * 2 + h], around("aux", -1))

    ints_step(0)
    for d in (1, 7, 2, 6, 3, 5, 4):
        slot = occ_all.at[block(-d)]
        arrive(("o", d), slot)
        post(("os", d), slot, slot, sibling)
    ints_step(1)
    for d in (0, 1, 7, 2, 6, 3, 5, 4):
        arrive(("os", d), occ_all.at[block(-d, False)])

    pieces = []
    for rel in (0, -1, 1, 2):
        first = pl.multiple_of(((x + rel + nx) % nx) * rows, rows)
        for k in range(slots):
            live = jnp.where(k < count[0], 1.0, 0.0).astype(jnp.float32)
            picked = occ_all[partner[0, k], pl.ds(first, rows), :].astype(jnp.float32)
            pieces.append(picked * live)
    spread[...] = jnp.concatenate(pieces, axis=0).T.astype(jnp.bfloat16)

    def half_step(c):
        arrive(("x", "D", c), from_far.at[part(c)])
        columns = []
        for p in range(firsts[c], firsts[c] + sizes[c]):
            columns.append(
                jnp.concatenate(
                    [
                        ref[p].reshape(slots * rows, width)
                        for ref in (ints, from_left, from_right, from_far)
                    ],
                    axis=0,
                )
            )
        res = jnp.dot(
            spread[...], jnp.concatenate(columns, axis=1), preferred_element_type=jnp.float32
        ).astype(jnp.bfloat16)
        for j in range(sizes[c]):
            half[me, firsts[c] + j] = res[:, j * width : (j + 1) * width]
        own = half.at[me, part(c)]
        post(("y", "R", 1, c), own, own, around("ao", 1))
        post(("y", "L", 1, c), own, own, around("ao", -1))
        post(("s", "O", 0, c), own, own, sibling)

    def routes(d, c):
        far = ny // 2
        if d < far:
            return ("R", "L")
        if d > far:
            return ()
        return ("R",) if c % 2 == 0 else ("L",)

    def half_pass(d, c):
        for way in routes(d, c):
            sign = 1 if way == "R" else -1
            slot = half.at[block(-sign * d), part(c)]
            arrive(("y", way, d, c), slot)
            if way in routes(d + 1, c):
                post(("y", way, d + 1, c), slot, slot, around("ao", sign))
            post(("s", way, d, c), slot, slot, sibling)

    def vir_pass(d):
        for h in range(2):
            for way in routes(d, h):
                sign = 1 if way == "R" else -1
                slot = vir_all.at[((z - sign * d + nz) % nz) * 2 + h]
                arrive(("v", way, d, h), slot)
                if way in routes(d + 1, h):
                    post(("v", way, d + 1, h), slot, slot, around("aux", sign))

    def mask():
        def body(m, carry):
            for b in range(vdom.shape[0]):
                on = jnp.full((width, width), vdom[b, m].astype(jnp.float32)).astype(jnp.bfloat16)
                at = slice(b * width, (b + 1) * width)
                first = pl.multiple_of(m * width, width)
                vir_masked[pl.ds(first, width), at] = vir_all[m, :, at] * on
            return carry

        lax.fori_loop(0, vir_all.shape[0], body, 0)

    def drain(c, near=True, last=True):
        if near:
            arrive(("s", "O", 0, c), half.at[block(0, False), part(c)])
        for d in range(1 if near else ny // 2, ny // 2 + (1 if last else 0)):
            for way in routes(d, c):
                sign = 1 if way == "R" else -1
                arrive(("s", way, d, c), half.at[block(-sign * d, False), part(c)])

    def multiply(c):
        blocks = half.shape[0]

        def body(t, carry):
            p = firsts[c] + t * 2
            lhs = jnp.concatenate(
                [half[n, pl.ds(p, 2)].reshape(2 * width, width) for n in range(blocks)], axis=1
            )
            res = jnp.dot(lhs, vir_masked[...], preferred_element_type=jnp.float32)
            staged[pl.ds(p, 2)] = res.astype(jnp.bfloat16).reshape(2, width, -1)
            return carry

        lax.fori_loop(0, sizes[c] // 2, body, 0)
        done = pltpu.make_async_copy(staged.at[part(c)], out.at[part(c)], out_sem.at[c])
        done.start()
        return done

    def pair(delta, p):
        there = (y + delta + ny) % ny
        lhs = [half[there * 2 + n, pl.ds(p, 2)].reshape(2 * width, width) for n in range(2)]
        rows_at = pl.multiple_of(there * 2 * width, 2 * width)
        return lhs, vir_masked[pl.ds(rows_at, 2 * width), :]

    def multiply_near(c):
        def body(t, carry):
            lhs, rhs = [], []
            for delta in range(1 - ny // 2, ny // 2):
                a, b = pair(delta, firsts[c] + t * 2)
                lhs += a
                rhs.append(b)
            total[t] = jnp.dot(
                jnp.concatenate(lhs, axis=1), jnp.concatenate(rhs, axis=0),
                preferred_element_type=jnp.float32,
            )
            return carry

        lax.fori_loop(0, sizes[c] // 2, body, 0)

    def multiply_far(c):
        def body(t, carry):
            p = firsts[c] + t * 2
            lhs, rhs = pair(ny // 2, p)
            res = total[t] + jnp.dot(
                jnp.concatenate(lhs, axis=1), rhs, preferred_element_type=jnp.float32
            )
            staged[pl.ds(p, 2)] = res.astype(jnp.bfloat16).reshape(2, width, -1)
            return carry

        lax.fori_loop(0, sizes[c] // 2, body, 0)
        done = pltpu.make_async_copy(staged.at[part(c)], out.at[part(c)], out_sem.at[c])
        done.start()
        return done

    outs = []
    far = ny // 2
    for s in range(chunks + far):
        if 1 < s + 1 < chunks:
            ints_step(s + 1)
        if s < chunks:
            half_step(s)
        for d in range(1, far + 1):
            if 0 <= s - d < chunks:
                half_pass(d, s - d)
        for d in range(1, far + 1):
            if s == vir_steps[d - 1]:
                vir_pass(d)
        if s == vir_steps[-1]:
            mask()
        if s >= max(far, vir_steps[-1]):
            while len(outs) <= s - far:
                if len(outs) == chunks - 1:
                    drain(chunks - 1, near=False)
                    outs.append(multiply_far(chunks - 1))
                else:
                    drain(len(outs))
                    outs.append(multiply(len(outs)))
        if s == chunks + far - 2:
            drain(chunks - 1, last=False)
            multiply_near(chunks - 1)
    for c in pending:
        c.wait_send()
    for c in outs:
        c.wait()


def copies(chunks):
    return 18 * chunks + 29


def local(size, integrals, partner, pair_count, occ_coeff, occ_domain, vir_coeff, vir_domain):
    slab, _, slots, rows, width = integrals.shape
    nz, ny, nx = size
    blocks = 2 * ny
    occ_width = occ_coeff.shape[1]
    vir_width = vir_coeff.shape[1]
    ints = integrals.reshape(slab, slots, rows, width)
    vir = vir_coeff.reshape(-1, width, vir_width)
    n = copies(len(CHUNKS))
    vmem = pl.BlockSpec(memory_space=pltpu.VMEM)
    smem = pl.BlockSpec(memory_space=pltpu.SMEM)
    return pl.pallas_call(
        functools.partial(kernel, size, CHUNKS, VIR_STEPS),
        out_shape=jax.ShapeDtypeStruct((slab, occ_width, vir_width), jnp.bfloat16),
        in_specs=[vmem] * 3 + [smem] * 4,
        out_specs=pl.BlockSpec(memory_space=pl.ANY),
        scratch_shapes=[
            pltpu.VMEM((blocks, width, occ_width), jnp.bfloat16),
            pltpu.VMEM(ints.shape, jnp.bfloat16),
            pltpu.VMEM(ints.shape, jnp.bfloat16),
            pltpu.VMEM(ints.shape, jnp.bfloat16),
            pltpu.VMEM((occ_width, nx * slots * rows), jnp.bfloat16),
            pltpu.VMEM((blocks, slab, occ_width, width), jnp.bfloat16),
            pltpu.VMEM((blocks, width, vir_width), jnp.bfloat16),
            pltpu.VMEM((blocks * width, vir_width), jnp.bfloat16),
            pltpu.VMEM((slab, occ_width, vir_width), jnp.bfloat16),
            pltpu.VMEM((CHUNKS[-1] // 2, 2 * width, vir_width), jnp.float32),
            pltpu.SemaphoreType.DMA((n,)),
            pltpu.SemaphoreType.DMA((n,)),
            pltpu.SemaphoreType.DMA((len(CHUNKS),)),
        ],
        compiler_params=pltpu.CompilerParams(
            collective_id=0, has_side_effects=True, vmem_limit_bytes=30 * 1024 * 1024
        ),
    )(occ_coeff, ints, vir, partner, pair_count, occ_domain, vir_domain.T)


def solution(mesh):
    size = (mesh.shape["aux"], mesh.shape["ao"] // 2, mesh.shape["orb"])
    placed = (
        P("aux", "ao", None, "orb", None),
        P("ao", None),
        P("ao"),
        P("ao", "orb"),
        P("ao", "orb"),
        P("aux", "ao"),
        P(None, "ao"),
    )
    return jax.shard_map(
        functools.partial(local, size), mesh=mesh, in_specs=placed,
        out_specs=P("aux", "orb", "ao"), check_vma=False,
    )
```
